512 devices in a mesh: aux: 32 (over x, z), row: 16 (over y, core).
Axes of the slice: x: 4, y: 8, z: 8, core: 2. Of those that a mesh axis runs over, the one named last changes fastest.
Arguments:
- slabs: bfloat16 [256, 400, 2048], P('aux', None, 'row'), may hold values from -0.33398438 to 0.33398438
- significant: int32 [256, 32], P('aux'), may hold values from 0 to 1, as said below
Outputs:
- exchange: float32 [2048, 2048], P('row', 'aux')
The draws below stay inside these ranges and needn't reach their ends.
Inputs may be any that keep to these rules, and one draw needn't show every extreme that they name: `significant`: each entry is 0 or 1; the share of ones differs between the auxiliary functions of different devices.
All inputs are finite; a program needn't handle non-finite values.
Results may differ from the reference program's by a relative error of at most 0.0003.
Values may be sent and summed in bfloat16 or wider, within the bound.
No kernel may reach another device: no remote copies, remote signals or barrier semaphores. Data moves between devices by JAX's collectives and lax.ppermute only.
A program may use at most 64 MiB of HBM per device.

```python
import jax
import jax.numpy as jnp
from jax import lax

NBF = 2048
NOCC = 400
BS = 64
AUX_DEV = 8
NAUXW = 256
NBLK = 32


def draw_significant(key, part):
    first_key, second_key = jax.random.split(jax.random.fold_in(key, 11))
    groups = NAUXW // AUX_DEV
    levels = jax.random.randint(first_key, (groups, 1, 1), 3, 19)
    levels = jnp.broadcast_to(levels, (groups, AUX_DEV, NBLK)).reshape(NAUXW, NBLK)
    rolled = jax.random.randint(second_key, (NAUXW, NBLK), 0, 20)
    return (rolled < levels).astype(jnp.int32)


def block_levels(own_key, extent, cuts, low, largest):
    def one(position, blocks):
        draws = jax.random.uniform(jax.random.fold_in(jax.random.fold_in(own_key, 6), position), (blocks,), jnp.float32, low / len(cuts), largest / len(cuts))
        return jnp.repeat(jnp.exp(draws), extent[position] // blocks).reshape((-1,) + (1,) * (len(extent) - position - 1))

    level = one(*cuts[0])
    for cut in cuts[1:]:
        level = level * one(*cut)
    return level


def scatter_about(rng, extent, scale, most, cuts=(), held_as=jnp.bfloat16):
    level = block_levels(rng, extent, cuts, -0.22, 0.18) if cuts else 1.0
    entries = jax.random.normal(rng, extent, jnp.float32) * scale * level
    return jnp.minimum(jnp.maximum(entries, -most), most).astype(held_as)


def setup_inputs(seed: int = 0) -> dict:
    key_of = jax.random.split(jax.random.key(seed), 3)
    return {
        "slabs": scatter_about(key_of[0], (NAUXW, NOCC, NBF), ((NAUXW * NOCC) ** -0.25), 0.33398438, ((0, 32), (2, 16))),
        "significant": draw_significant(jax.random.fold_in(key_of[2], 71), 0),
    }


def reference(slabs, significant):
    block_of = lax.broadcasted_iota(jnp.int32, (NBLK, NBF), 1) // BS
    block_id = lax.broadcasted_iota(jnp.int32, (NBLK, NBF), 0)
    expand_table = (block_of == block_id).astype(jnp.float32)
    column_mask = jnp.dot(significant.astype(jnp.float32), expand_table).astype(jnp.bfloat16)
    masked = (slabs * column_mask[:, None, :]).reshape(NAUXW * NOCC, NBF)
    return lax.dot_general(masked, masked, (((0,), (0,)), ((), ())), preferred_element_type=jnp.float32)
```

```python
import jax
import jax.numpy as jnp
from jax import lax
from jax.sharding import PartitionSpec as P

BS = 64
AX, AZ = 4, 8
CHIPS = 8


def dev(aux, chip, core):
    return aux * 2 * CHIPS + (chip % CHIPS) * 2 + core


def block_at(core, step, row, col):
    return 2 + 4 * (step - 1) + 2 * (col != core) + (row != core)


def sources(X, j, Y, i):
    d = (X - Y) % CHIPS
    if d == 0:
        return ((i, 0), None) if i == j else ((i, 1), (j, 1))
    if d == CHIPS // 2:
        if i != j:
            return (i, 14), (j, 14)
        low = Y < CHIPS // 2
        return (i if low else 1 - i, 15), (1 - i if low else i, 15)
    s, up = (d, 1) if d < CHIPS // 2 else (CHIPS - d, 0)
    return (up, block_at(up, s, i, j)), (1 - up, block_at(1 - up, s, j, i))


def deliveries():
    direct = ([], [])
    mirrored = []
    for A in range(AX * AZ):
        X, j, h = A // 4, A // 2 % 2, A % 2
        for Y in range(CHIPS):
            for i in range(2):
                own, other = sources(X, j, Y, i)
                for p in range(2):
                    direct[p].append((dev(2 * own[1] + (h ^ p), Y, own[0]), dev(A, Y, i)))
                if other is not None:
                    mirrored.append((dev(2 * other[1] + h, X, other[0]), dev(A, Y, i)))
    return direct[0], direct[1], mirrored


def local(slabs, significant):
    aux_here, occupied, cols = slabs.shape
    half = aux_here // 2
    depth = half * occupied
    row = lax.axis_index("row")
    aux = lax.axis_index("aux")
    chip, core = row // 2, row % 2

    blocks = cols // BS
    mine = lax.dynamic_slice_in_dim(significant, row * blocks, blocks, 1)
    lane = lax.broadcasted_iota(jnp.int32, (aux_here, cols), 1) // BS
    keep = jnp.where(lane == 0, mine[:, :1], mine[:, 1:2]) != 0
    masked = jnp.where(keep[:, None, :], slabs, jnp.zeros_like(slabs))

    own = lax.dynamic_slice_in_dim(masked, core * half, half, 0).reshape(depth, cols)
    give = lax.dynamic_slice_in_dim(masked, (1 - core) * half, half, 0).reshape(depth, cols)
    swap = [(r, r ^ 1) for r in range(2 * CHIPS)]
    ring = [
        (2 * y + c, 2 * ((y + (1 if c == 0 else -1)) % CHIPS) + c)
        for y in range(CHIPS)
        for c in range(2)
    ]
    a, b = own, lax.ppermute(give, "row", swap)
    left = jnp.concatenate([own.T, b.T], axis=0)
    whole = masked.reshape(2 * depth, cols)

    def dot(x, y):
        return jnp.dot(x, y, preferred_element_type=jnp.float32)

    made = [dot(whole.T, whole), dot(own.T, b)]
    for step in range(1, CHIPS // 2 + 1):
        a = lax.ppermute(a, "row", ring)
        b = lax.ppermute(b, "row", ring)
        if step < CHIPS // 2:
            made += [dot(left, a), dot(left, b)]
        else:
            low = chip < CHIPS // 2
            made.append(dot(left[:cols], b))
            made.append(dot(jnp.where(low, left[:cols], left[cols:]), jnp.where(low, a, b)))
    pieces = jnp.concatenate(made, axis=0).reshape(AX, AZ, BS, cols)

    over_x = [[x * AZ + z for x in range(AX)] for z in range(AZ)]
    over_z = [[x * AZ + z for z in range(AZ)] for x in range(AX)]
    got = lax.all_to_all(pieces, "aux", 0, 0, axis_index_groups=over_x, tiled=True).sum(axis=0)
    got = lax.all_to_all(got, "aux", 0, 0, axis_index_groups=over_z, tiled=True).sum(axis=0)

    first, second, mirrored = deliveries()
    d0 = lax.ppermute(got, ("aux", "row"), first)
    d1 = lax.ppermute(got, ("aux", "row"), second)
    t = lax.ppermute(got, ("aux", "row"), mirrored)
    odd = aux % 2 == 1
    whole_rows = jnp.concatenate([jnp.where(odd, d1, d0), jnp.where(odd, d0, d1)], axis=0)
    direct = jnp.where(odd, whole_rows[:, BS:], whole_rows[:, :BS])
    return direct + t.T


def solution(mesh):
    return jax.shard_map(
        local,
        mesh=mesh,
        in_specs=(P("aux", None, "row"), P("aux", None)),
        out_specs=P("row", "aux"),
        check_vma=False,
    )
```

```python
import jax
import jax.numpy as jnp
from jax import lax
from jax.sharding import PartitionSpec as P

BS = 64
AX, AZ = 4, 8
CHIPS = 8


def dev(aux, chip, core):
    return aux * 2 * CHIPS + (chip % CHIPS) * 2 + core


def block_at(core, step, row, col):
    return 2 + 4 * (step - 1) + 2 * (col != core) + (row != core)


def sources(X, j, Y, i):
    d = (X - Y) % CHIPS
    if d == 0:
        return ((i, 0), None) if i == j else ((i, 1), (j, 1))
    if d == CHIPS // 2:
        if i != j:
            return (i, 14), (j, 14)
        low = Y < CHIPS // 2
        return (i if low else 1 - i, 15), (1 - i if low else i, 15)
    s, up = (d, 1) if d < CHIPS // 2 else (CHIPS - d, 0)
    return (up, block_at(up, s, i, j)), (1 - up, block_at(1 - up, s, j, i))


PARTS = (10, 4, 2)


def holder(place, g):
    first, z = 0, 0
    for count in PARTS:
        each = 2 * count // AX
        if place < first + count:
            x, k = divmod(2 * (place - first) + g, each)
            return x * AZ + z + k
        first, z = first + count, z + each


def deliveries():
    direct = ([], [])
    mirrored = []
    for A in range(AX * AZ):
        X, j, h = A // 4, A // 2 % 2, A % 2
        for Y in range(CHIPS):
            for i in range(2):
                own, other = sources(X, j, Y, i)
                for p in range(2):
                    direct[p].append((dev(holder(own[1], h ^ p), Y, own[0]), dev(A, Y, i)))
                if other is not None:
                    mirrored.append((dev(holder(other[1], h), X, other[0]), dev(A, Y, i)))
    return direct[0], direct[1], mirrored


def local(slabs, significant):
    aux_here, occupied, cols = slabs.shape
    half = aux_here // 2
    depth = half * occupied
    row = lax.axis_index("row")
    aux = lax.axis_index("aux")
    chip, core = row // 2, row % 2

    blocks = cols // BS
    mine = lax.dynamic_slice_in_dim(significant, row * blocks, blocks, 1)
    lane = lax.broadcasted_iota(jnp.int32, (aux_here, cols), 1) // BS
    keep = jnp.where(lane == 0, mine[:, :1], mine[:, 1:2]) != 0
    masked = jnp.where(keep[:, None, :], slabs, jnp.zeros_like(slabs))

    own = lax.dynamic_slice_in_dim(masked, core * half, half, 0).reshape(depth, cols)
    give = lax.dynamic_slice_in_dim(masked, (1 - core) * half, half, 0).reshape(depth, cols)
    swap = [(r, r ^ 1) for r in range(2 * CHIPS)]
    ring = [
        (2 * y + c, 2 * ((y + (1 if c == 0 else -1)) % CHIPS) + c)
        for y in range(CHIPS)
        for c in range(2)
    ]
    a, b = own, lax.ppermute(give, "row", swap)
    left = jnp.concatenate([own.T, b.T], axis=0)
    whole = masked.reshape(2 * depth, cols)

    def dot(x, y):
        return jnp.dot(x, y, preferred_element_type=jnp.float32)

    over_x = [[x * AZ + z for x in range(AX)] for z in range(AZ)]

    def sum_over_x(blocks):
        parts = jnp.concatenate(blocks, axis=0).reshape(AX, -1, BS, cols)
        return lax.all_to_all(parts, "aux", 0, 0, axis_index_groups=over_x, tiled=True).sum(axis=0)

    made = [dot(whole.T, whole), dot(own.T, b)]
    for _ in range(2):
        a, b = lax.ppermute(a, "row", ring), lax.ppermute(b, "row", ring)
        made += [dot(left, a), dot(left, b)]
    sums = [sum_over_x(made)]
    a, b = lax.ppermute(a, "row", ring), lax.ppermute(b, "row", ring)
    a, b, sums[0] = lax.optimization_barrier((a, b, sums[0]))
    made = [dot(left, a), dot(left, b)]
    a, b = lax.ppermute(a, "row", ring), lax.ppermute(b, "row", ring)
    sums.append(sum_over_x(made))
    a, b, sums[1] = lax.optimization_barrier((a, b, sums[1]))
    low = chip < CHIPS // 2
    near = jnp.where(low, left[:cols], left[cols:])
    sums.append(sum_over_x([dot(left[:cols], b), dot(near, jnp.where(low, a, b))]))

    over_z = [[x * AZ + z for z in range(AZ)] for x in range(AX)]
    got = jnp.concatenate(sums, axis=0)
    got = lax.all_to_all(got, "aux", 0, 0, axis_index_groups=over_z, tiled=True).sum(axis=0)

    first, second, mirrored = deliveries()
    d0 = lax.ppermute(got, ("aux", "row"), first)
    d1 = lax.ppermute(got, ("aux", "row"), second)
    t = lax.ppermute(got, ("aux", "row"), mirrored)
    odd = aux % 2 == 1
    whole_rows = jnp.concatenate([jnp.where(odd, d1, d0), jnp.where(odd, d0, d1)], axis=0)
    direct = jnp.where(odd, whole_rows[:, BS:], whole_rows[:, :BS])
    return direct + t.T


def solution(mesh):
    return jax.shard_map(
        local,
        mesh=mesh,
        in_specs=(P("aux", None, "row"), P("aux", None)),
        out_specs=P("row", "aux"),
        check_vma=False,
    )
```

```python
import jax
import jax.numpy as jnp
from jax import lax
from jax.sharding import PartitionSpec as P

BS = 64
AX, AZ = 4, 8
CHIPS = 8


def dev(aux, chip, core):
    return aux * 2 * CHIPS + (chip % CHIPS) * 2 + core


def block_at(core, step, row, col):
    return 2 + 4 * (step - 1) + 2 * (col != core) + (row != core)


def sources(X, j, Y, i):
    d = (X - Y) % CHIPS
    if d == 0:
        return ((i, 0), None) if i == j else ((i, 1), (j, 1))
    if d == CHIPS // 2:
        if i != j:
            return (i, 14), (j, 14)
        low = Y < CHIPS // 2
        return (i if low else 1 - i, 15), (1 - i if low else i, 15)
    s, up = (d, 1) if d < CHIPS // 2 else (CHIPS - d, 0)
    return (up, block_at(up, s, i, j)), (1 - up, block_at(1 - up, s, j, i))


def holder(place, g):
    first, second = divmod(2 * place + g, AZ // 2)
    return first // 2 * AZ + 2 * second + first % 2


def deliveries():
    direct = ([], [])
    mirrored = []
    for A in range(AX * AZ):
        X, j, h = A // 4, A // 2 % 2, A % 2
        for Y in range(CHIPS):
            for i in range(2):
                own, other = sources(X, j, Y, i)
                for p in range(2):
                    direct[p].append((dev(holder(own[1], h ^ p), Y, own[0]), dev(A, Y, i)))
                if other is not None:
                    mirrored.append((dev(holder(other[1], h), X, other[0]), dev(A, Y, i)))
    return direct[0], direct[1], mirrored


def local(slabs, significant):
    aux_here, occupied, cols = slabs.shape
    half = aux_here // 2
    depth = half * occupied
    row = lax.axis_index("row")
    aux = lax.axis_index("aux")
    chip, core = row // 2, row % 2

    blocks = cols // BS
    lane = lax.broadcasted_iota(jnp.int32, (1, cols), 1) // BS

    def mask_of(first, count, block_row):
        mine = lax.dynamic_slice(significant, (first, block_row * blocks), (count, blocks))
        return (jnp.where(lane == 0, mine[:, :1], mine[:, 1:2]) != 0)[:, None, :]

    def masked_half(x, block_row):
        x = x.reshape(half, occupied, cols)
        return jnp.where(mask_of(core * half, half, block_row), x, jnp.zeros_like(x)).reshape(depth, cols)

    masked = jnp.where(mask_of(0, aux_here, row), slabs, jnp.zeros_like(slabs))
    raw = lax.dynamic_slice_in_dim(slabs, core * half, half, 0).reshape(depth, cols)
    own = lax.dynamic_slice_in_dim(masked, core * half, half, 0).reshape(depth, cols)
    give = lax.dynamic_slice_in_dim(masked, (1 - core) * half, half, 0).reshape(depth, cols)
    swap = [(r, r ^ 1) for r in range(2 * CHIPS)]
    ring = [
        (2 * y + c, 2 * ((y + (1 if c == 0 else -1)) % CHIPS) + c)
        for y in range(CHIPS)
        for c in range(2)
    ]
    a, b = raw, lax.ppermute(give, "row", swap)
    left = jnp.concatenate([own.T, b.T], axis=0)
    whole = masked.reshape(2 * depth, cols)

    def dot(x, y):
        return jnp.dot(x, y, preferred_element_type=jnp.float32)

    made = [dot(whole.T, whole), dot(own.T, b)]
    for step in range(1, CHIPS // 2 + 1):
        a = lax.ppermute(a, "row", ring)
        b = lax.ppermute(b, "row", ring)
        there = (chip + jnp.where(core == 0, CHIPS - step, step)) % CHIPS
        near = masked_half(a, 2 * there + core)
        if step < CHIPS // 2:
            made += [dot(left, near), dot(left, b)]
        else:
            low = chip < CHIPS // 2
            made.append(dot(left[:cols], b))
            made.append(dot(jnp.where(low, left[:cols], left[cols:]), jnp.where(low, near, b)))
    pieces = jnp.concatenate(made, axis=0).reshape(2 * AX, AZ // 2, BS, cols)

    eights = [[x * AZ + 2 * k + m for x in range(AX) for m in range(2)] for k in range(AZ // 2)]
    fours = [[x * AZ + 2 * k + m for k in range(AZ // 2)] for x in range(AX) for m in range(2)]
    got = lax.all_to_all(pieces, "aux", 0, 0, axis_index_groups=eights, tiled=True).sum(axis=0)
    got = lax.all_to_all(got, "aux", 0, 0, axis_index_groups=fours, tiled=True).sum(axis=0)

    first, second, mirrored = deliveries()
    d0 = lax.ppermute(got, ("aux", "row"), first)
    d1 = lax.ppermute(got, ("aux", "row"), second)
    t = lax.ppermute(got, ("aux", "row"), mirrored)
    odd = aux % 2 == 1
    whole_rows = jnp.concatenate([jnp.where(odd, d1, d0), jnp.where(odd, d0, d1)], axis=0)
    direct = jnp.where(odd, whole_rows[:, BS:], whole_rows[:, :BS])
    return direct + t.T


def solution(mesh):
    return jax.shard_map(
        local,
        mesh=mesh,
        in_specs=(P("aux", None, "row"), P("aux", None)),
        out_specs=P("row", "aux"),
        check_vma=False,
    )
```

```python
import jax
import jax.numpy as jnp
from jax import lax
from jax.sharding import PartitionSpec as P

BS = 64
AX, AZ = 4, 8
CHIPS = 8


def dev(aux, chip, core):
    return aux * 2 * CHIPS + (chip % CHIPS) * 2 + core


def block_at(core, step, row, col):
    return 2 + 4 * (step - 1) + 2 * (col != core) + (row != core)


def sources(X, j, Y, i):
    d = (X - Y) % CHIPS
    if d == 0:
        return ((i, 0), None) if i == j else ((i, 1), (j, 1))
    if d == CHIPS // 2:
        if i != j:
            return (i, 14), (j, 14)
        low = Y < CHIPS // 2
        return (i if low else 1 - i, 15), (1 - i if low else i, 15)
    s, up = (d, 1) if d < CHIPS // 2 else (CHIPS - d, 0)
    return (up, block_at(up, s, i, j)), (1 - up, block_at(1 - up, s, j, i))


def holder(place, g):
    first, second = divmod(2 * place + g, AZ // 2)
    return first // 2 * AZ + 2 * second + first % 2


def deliveries():
    direct = ([], [])
    mirrored = []
    for A in range(AX * AZ):
        X, j, h = A // 4, A // 2 % 2, A % 2
        for Y in range(CHIPS):
            for i in range(2):
                own, other = sources(X, j, Y, i)
                for p in range(2):
                    direct[p].append((dev(holder(own[1], h ^ p), Y, own[0]), dev(A, Y, i)))
                if other is not None:
                    mirrored.append((dev(holder(other[1], h), X, other[0]), dev(A, Y, i)))
    return direct[0], direct[1], mirrored


def local(slabs, significant):
    aux_here, occupied, cols = slabs.shape
    half = aux_here // 2
    depth = half * occupied
    row = lax.axis_index("row")
    aux = lax.axis_index("aux")
    chip, core = row // 2, row % 2

    blocks = cols // BS
    lane = lax.broadcasted_iota(jnp.int32, (1, cols), 1) // BS

    def mask_of(first, count, block_row):
        mine = lax.dynamic_slice(significant, (first, block_row * blocks), (count, blocks))
        return (jnp.where(lane == 0, mine[:, :1], mine[:, 1:2]) != 0)[:, None, :]

    def masked_half(x, block_row, which=core):
        x = x.reshape(half, occupied, cols)
        return jnp.where(mask_of(which * half, half, block_row), x, jnp.zeros_like(x)).reshape(depth, cols)

    def raw_half(which):
        return lax.dynamic_slice_in_dim(slabs, which * half, half, 0).reshape(depth, cols)

    swap = [(r, r ^ 1) for r in range(2 * CHIPS)]
    ring = [
        (2 * y + c, 2 * ((y + (1 if c == 0 else -1)) % CHIPS) + c)
        for y in range(CHIPS)
        for c in range(2)
    ]
    cross = [(2 * y + 1 - c, 2 * ((y + (1 if c == 0 else -1)) % CHIPS) + c) for y in range(CHIPS) for c in range(2)]
    a, b = lax.optimization_barrier((raw_half(core), raw_half(1 - core)))
    far_a, far_b = lax.ppermute(a, "row", ring), lax.ppermute(b, "row", cross)
    masked = jnp.where(mask_of(0, aux_here, row), slabs, jnp.zeros_like(slabs))
    own = masked_half(a, row)
    other = lax.ppermute(masked_half(b, row, 1 - core), "row", swap)
    left = jnp.concatenate([own.T, other.T], axis=0)
    whole = masked.reshape(2 * depth, cols)

    def dot(x, y):
        return jnp.dot(x, y, preferred_element_type=jnp.float32)

    made = [dot(whole.T, whole), dot(own.T, other)]
    for step in range(1, CHIPS // 2 + 1):
        there = (chip + jnp.where(core == 0, CHIPS - step, step)) % CHIPS
        near_a = masked_half(far_a, 2 * there + core)
        near_b = masked_half(far_b, 2 * there + 1 - core)
        if step < CHIPS // 2:
            far_a, far_b = lax.ppermute(far_a, "row", ring), lax.ppermute(far_b, "row", ring)
            made += [dot(left, near_a), dot(left, near_b)]
        else:
            low = chip < CHIPS // 2
            made.append(dot(left[:cols], near_b))
            made.append(dot(jnp.where(low, left[:cols], left[cols:]), jnp.where(low, near_a, near_b)))
    pieces = jnp.concatenate(made, axis=0).reshape(2 * AX, AZ // 2, BS, cols)

    eights = [[x * AZ + 2 * k + m for x in range(AX) for m in range(2)] for k in range(AZ // 2)]
    fours = [[x * AZ + 2 * k + m for k in range(AZ // 2)] for x in range(AX) for m in range(2)]
    got = lax.all_to_all(pieces, "aux", 0, 0, axis_index_groups=eights, tiled=True).sum(axis=0)
    got = lax.all_to_all(got, "aux", 0, 0, axis_index_groups=fours, tiled=True).sum(axis=0)

    first, second, mirrored = deliveries()
    d0 = lax.ppermute(got, ("aux", "row"), first)
    d1 = lax.ppermute(got, ("aux", "row"), second)
    t = lax.ppermute(got, ("aux", "row"), mirrored)
    odd = aux % 2 == 1
    whole_rows = jnp.concatenate([jnp.where(odd, d1, d0), jnp.where(odd, d0, d1)], axis=0)
    direct = jnp.where(odd, whole_rows[:, BS:], whole_rows[:, :BS])
    return direct + t.T


def solution(mesh):
    return jax.shard_map(
        local,
        mesh=mesh,
        in_specs=(P("aux", None, "row"), P("aux", None)),
        out_specs=P("row", "aux"),
        check_vma=False,
    )
```

```python
import jax
import jax.numpy as jnp
from jax import lax
from jax.sharding import PartitionSpec as P

BS = 64
AX, AZ = 4, 8
CHIPS = 8
BOTH = ("aux", "row")


def dev(aux, chip, core):
    return aux * 2 * CHIPS + (chip % CHIPS) * 2 + core


PLACES = {(s, e, f): (s - 1, f, e) for s in range(1, CHIPS // 2) for f in range(2) for e in range(2)}
PLACES |= {(s, 0, f): (3, s // 4, f) for s in (0, 4) for f in range(2)}


ORDER = [(3, 0)] + [(pair, m) for pair in range(3) for m in range(2)] + [(3, 1)]


def first_holder(Y, core, pair):
    if core:
        return (Y + 1 + 2 * pair) % CHIPS // 2
    return (Y - 1 - 2 * pair) % CHIPS // 2


def second_holder(Y, q, g):
    return 2 * ((Y + q) % 2) + g


def holder(Y, core, tile, g):
    pair, m, q = PLACES[tile]
    return dev(first_holder(Y, core, pair) * AZ + 2 * second_holder(Y, q, g) + (core ^ m), Y, core)


def summing_groups():
    rows = [(Y, c) for Y in range(CHIPS) for c in range(2)]
    first = [
        [dev(first_holder(Y, c, pair) * AZ + 2 * k + (c ^ m), Y, c) for pair, m in ORDER]
        for k in range(AZ // 2)
        for Y, c in rows
    ]
    second = [
        [dev(x * AZ + 2 * second_holder(Y, q, g) + m, Y, c) for q in range(2) for g in range(2)]
        for x in range(AX)
        for m in range(2)
        for Y, c in rows
    ]
    return first, second


def sources(X, j, Y, i):
    d = (X - Y) % CHIPS
    if d == 0:
        return ((i, (0, 0, 0)), None) if i == j else ((i, (0, 0, 1)), (j, (0, 0, 1)))
    if d == CHIPS // 2:
        if i != j:
            return (i, (4, 0, 1)), (j, (4, 0, 1))
        low = Y < CHIPS // 2
        return (i if low else 1 - i, (4, 0, 0)), (1 - i if low else i, (4, 0, 0))
    s, here = (d, 1) if d < CHIPS // 2 else (CHIPS - d, 0)
    there = 1 - here
    return (here, (s, int(i != here), int(j != here))), (there, (s, int(j != there), int(i != there)))


def deliveries():
    direct = ([], [])
    mirrored = []
    for A in range(AX * AZ):
        X, j, h = A // 4, A // 2 % 2, A % 2
        for Y in range(CHIPS):
            for i in range(2):
                own, other = sources(X, j, Y, i)
                for p in range(2):
                    direct[p].append((holder(Y, *own, h ^ p), dev(A, Y, i)))
                if other is not None:
                    mirrored.append((holder(X, *other, h), dev(A, Y, i)))
    return direct[0], direct[1], mirrored


def local(slabs, significant):
    aux_here, occupied, cols = slabs.shape
    half = aux_here // 2
    depth = half * occupied
    row = lax.axis_index("row")
    aux = lax.axis_index("aux")
    chip, core = row // 2, row % 2

    blocks = cols // BS
    lane = lax.broadcasted_iota(jnp.int32, (1, cols), 1) // BS

    def mask_of(first, count, block_row):
        mine = lax.dynamic_slice(significant, (first, block_row * blocks), (count, blocks))
        return (jnp.where(lane == 0, mine[:, :1], mine[:, 1:2]) != 0)[:, None, :]

    def masked_half(x, block_row, which=core):
        x = x.reshape(half, occupied, cols)
        return jnp.where(mask_of(which * half, half, block_row), x, jnp.zeros_like(x)).reshape(depth, cols)

    def raw_half(which):
        return lax.dynamic_slice_in_dim(slabs, which * half, half, 0).reshape(depth, cols)

    swap = [(r, r ^ 1) for r in range(2 * CHIPS)]
    ring = [
        (2 * y + c, 2 * ((y + (1 if c == 0 else -1)) % CHIPS) + c)
        for y in range(CHIPS)
        for c in range(2)
    ]
    cross = [(2 * y + 1 - c, 2 * ((y + (1 if c == 0 else -1)) % CHIPS) + c) for y in range(CHIPS) for c in range(2)]
    a, b = lax.optimization_barrier((raw_half(core), raw_half(1 - core)))
    far_a, far_b = lax.ppermute(a, "row", ring), lax.ppermute(b, "row", cross)
    masked = jnp.where(mask_of(0, aux_here, row), slabs, jnp.zeros_like(slabs))
    own = masked_half(a, row)
    other = lax.ppermute(masked_half(b, row, 1 - core), "row", swap)
    left = jnp.concatenate([own.T, other.T], axis=0)
    whole = masked.reshape(2 * depth, cols)

    def dot(x, y):
        return jnp.dot(x, y, preferred_element_type=jnp.float32)

    tiles = [dot(whole.T, whole), dot(own.T, other)]
    for step in range(1, CHIPS // 2 + 1):
        there = (chip + jnp.where(core == 0, CHIPS - step, step)) % CHIPS
        near_a = masked_half(far_a, 2 * there + core)
        near_b = masked_half(far_b, 2 * there + 1 - core)
        if step < CHIPS // 2:
            far_a, far_b = lax.ppermute(far_a, "row", ring), lax.ppermute(far_b, "row", ring)
            tiles += [dot(left, near_a), dot(left, near_b)]
        else:
            low = chip < CHIPS // 2
            tiles.append(dot(jnp.where(low, left[:cols], left[cols:]), jnp.where(low, near_a, near_b)))
            tiles.append(dot(left[:cols], near_b))
    pieces = jnp.concatenate(tiles, axis=0).reshape(2 * AX, AZ // 2, BS, cols)

    first, second = summing_groups()
    got = lax.all_to_all(pieces, BOTH, 0, 0, axis_index_groups=first, tiled=True).sum(axis=0)
    got = lax.all_to_all(got, BOTH, 0, 0, axis_index_groups=second, tiled=True).sum(axis=0)

    near, next_to, mirrored = deliveries()
    t = lax.optimization_barrier(lax.ppermute(got, BOTH, mirrored).T)
    d0 = lax.ppermute(got, BOTH, near)
    d1 = lax.ppermute(got, BOTH, next_to)
    odd = aux % 2 == 1
    top = jnp.where(odd, d1[:, BS:], d0[:, :BS])
    bottom = jnp.where(odd, d0[:, BS:], d1[:, :BS])
    return jnp.concatenate([top, bottom], axis=0) + t


def solution(mesh):
    return jax.shard_map(
        local,
        mesh=mesh,
        in_specs=(P("aux", None, "row"), P("aux", None)),
        out_specs=P("row", "aux"),
        check_vma=False,
    )
```

```python
import jax
import jax.numpy as jnp
from jax import lax
from jax.sharding import PartitionSpec as P

BS = 64
AX, AZ = 4, 8
CHIPS = 8
BOTH = ("aux", "row")


def dev(aux, chip, core):
    return aux * 2 * CHIPS + (chip % CHIPS) * 2 + core


PLACES = {(0, 0): (0, 0), (1, 1): (0, 1), (2, 1): (1, 0), (3, 1): (1, 1)}
PLACES |= {(4, 0): (2, 0), (3, 0): (2, 1), (2, 0): (3, 0), (1, 0): (3, 1)}
PAIRS = [0, 3, 1, 2]


def first_holder(Y, core, pair):
    return (Y + (-2 * pair if core else 2 * pair)) % CHIPS // 2


def second_holder(Y, q, g):
    return 2 * ((Y + q) % 2) + g


def holder(Y, core, tile, g):
    pair, q = PLACES[tile[:2]]
    return dev(first_holder(Y, core, pair) * AZ + 2 * second_holder(Y, q, g) + (core ^ tile[2]), Y, core)


def summing_groups():
    rows = [(Y, c) for Y in range(CHIPS) for c in range(2)]
    first = [
        [dev(first_holder(Y, c, pair) * AZ + 2 * k + (c ^ m), Y, c) for pair in PAIRS for m in range(2)]
        for k in range(AZ // 2)
        for Y, c in rows
    ]
    second = []
    for x in range(AX):
        for m in range(2):
            for Y, c in rows:
                pair = next(p for p in PAIRS if first_holder(Y, c, p) == x)
                qs = (1, 0) if pair > 1 else (0, 1)
                second.append([dev(x * AZ + 2 * second_holder(Y, q, g) + m, Y, c) for q in qs for g in range(2)])
    return first, second


def sources(X, j, Y, i):
    d = (X - Y) % CHIPS
    if d == 0:
        return ((i, (0, 0, 0)), None) if i == j else ((i, (0, 0, 1)), (j, (0, 0, 1)))
    if d == CHIPS // 2:
        if i != j:
            return (i, (4, 0, 1)), (j, (4, 0, 1))
        low = Y < CHIPS // 2
        return (i if low else 1 - i, (4, 0, 0)), (1 - i if low else i, (4, 0, 0))
    s, here = (d, 1) if d < CHIPS // 2 else (CHIPS - d, 0)
    there = 1 - here
    return (here, (s, int(i != here), int(j != here))), (there, (s, int(j != there), int(i != there)))


def deliveries():
    direct = ([], [])
    mirrored = []
    for A in range(AX * AZ):
        X, j, h = A // 4, A // 2 % 2, A % 2
        for Y in range(CHIPS):
            for i in range(2):
                own, other = sources(X, j, Y, i)
                for p in range(2):
                    direct[p].append((holder(Y, *own, h ^ p), dev(A, Y, i)))
                if other is not None:
                    mirrored.append((holder(X, *other, h), dev(A, Y, i)))
    return direct[0], direct[1], mirrored


def local(slabs, significant):
    aux_here, occupied, cols = slabs.shape
    half = aux_here // 2
    depth = half * occupied
    row = lax.axis_index("row")
    aux = lax.axis_index("aux")
    chip, core = row // 2, row % 2

    blocks = cols // BS
    lane = lax.broadcasted_iota(jnp.int32, (1, cols), 1) // BS

    def mask_of(first, count, block_row):
        mine = lax.dynamic_slice(significant, (first, block_row * blocks), (count, blocks))
        return (jnp.where(lane == 0, mine[:, :1], mine[:, 1:2]) != 0)[:, None, :]

    def masked_half(x, block_row, which=core):
        x = x.reshape(half, occupied, cols)
        return jnp.where(mask_of(which * half, half, block_row), x, jnp.zeros_like(x)).reshape(depth, cols)

    def raw_half(which):
        return lax.dynamic_slice_in_dim(slabs, which * half, half, 0).reshape(depth, cols)

    swap = [(r, r ^ 1) for r in range(2 * CHIPS)]
    ring = [
        (2 * y + c, 2 * ((y + (1 if c == 0 else -1)) % CHIPS) + c)
        for y in range(CHIPS)
        for c in range(2)
    ]
    cross = [(2 * y + 1 - c, 2 * ((y + (1 if c == 0 else -1)) % CHIPS) + c) for y in range(CHIPS) for c in range(2)]
    a, b = lax.optimization_barrier((raw_half(core), raw_half(1 - core)))
    far_a, far_b = lax.ppermute(a, "row", ring), lax.ppermute(b, "row", cross)
    masked = jnp.where(mask_of(0, aux_here, row), slabs, jnp.zeros_like(slabs))
    own = masked_half(a, row)
    other = lax.ppermute(masked_half(b, row, 1 - core), "row", swap)
    left = (own.T, other.T)
    whole = masked.reshape(2 * depth, cols)

    def dot(x, y):
        return jnp.dot(x, y, preferred_element_type=jnp.float32)

    tiles = {(0, 0, 0): dot(whole.T, whole), (0, 0, 1): dot(left[0], other)}
    for step in range(1, CHIPS // 2 + 1):
        there = (chip + jnp.where(core == 0, CHIPS - step, step)) % CHIPS
        near_a = masked_half(far_a, 2 * there + core)
        near_b = masked_half(far_b, 2 * there + 1 - core)
        if step < CHIPS // 2:
            far_a, far_b = lax.ppermute(far_a, "row", ring), lax.ppermute(far_b, "row", ring)
            for e in range(2):
                tiles[step, e, 0], tiles[step, e, 1] = dot(left[e], near_a), dot(left[e], near_b)
        else:
            low = chip < CHIPS // 2
            tiles[4, 0, 0] = dot(jnp.where(low, left[0], left[1]), jnp.where(low, near_a, near_b))
            tiles[4, 0, 1] = dot(left[0], near_b)
    at = {place: tile for tile, place in PLACES.items()}
    pieces = [
        tiles[(*at[pair, q], m)] for pair in PAIRS for m in range(2) for q in ((1, 0) if pair > 1 else (0, 1))
    ]
    pieces = jnp.concatenate(pieces, axis=0).reshape(2 * AX, AZ // 2, BS, cols)

    first, second = summing_groups()
    got = lax.all_to_all(pieces, BOTH, 0, 0, axis_index_groups=first, tiled=True).sum(axis=0)
    got = lax.all_to_all(got, BOTH, 0, 0, axis_index_groups=second, tiled=True).sum(axis=0)

    near, next_to, mirrored = deliveries()
    t = lax.optimization_barrier(lax.ppermute(got, BOTH, mirrored).T)
    d0 = lax.ppermute(got, BOTH, near)
    d1 = lax.ppermute(got, BOTH, next_to)
    odd = aux % 2 == 1
    top = jnp.where(odd, d1[:, BS:], d0[:, :BS])
    bottom = jnp.where(odd, d0[:, BS:], d1[:, :BS])
    return jnp.concatenate([top, bottom], axis=0) + t


def solution(mesh):
    return jax.shard_map(
        local,
        mesh=mesh,
        in_specs=(P("aux", None, "row"), P("aux", None)),
        out_specs=P("row", "aux"),
        check_vma=False,
    )
```

```python
import functools
import itertools

import jax
import jax.numpy as jnp
from jax import lax
from jax.sharding import PartitionSpec as P

BS = 64
AX, AZ = 4, 8
CHIPS = 8
BOTH = ("aux", "row")


def dev(aux, chip, core):
    return aux * 2 * CHIPS + (chip % CHIPS) * 2 + core


PLACES = {(0, 0): (0, 0), (1, 1): (0, 1), (2, 1): (1, 0), (3, 1): (1, 1)}
PLACES |= {(4, 0): (2, 0), (3, 0): (2, 1), (2, 0): (3, 0), (1, 0): (3, 1)}
PAIRS = [0, 3, 1, 2]
POWER, MIRRORED = 2, 1.0


def sources(X, j, Y, i):
    d = (X - Y) % CHIPS
    if d == 0:
        return ((i, (0, 0, 0)), None) if i == j else ((i, (0, 0, 1)), (j, (0, 0, 1)))
    if d == CHIPS // 2:
        if i != j:
            return (i, (4, 0, 1)), (j, (4, 0, 1))
        low = Y < CHIPS // 2
        return (i if low else 1 - i, (4, 0, 0)), (1 - i if low else i, (4, 0, 0))
    s, here = (d, 1) if d < CHIPS // 2 else (CHIPS - d, 0)
    there = 1 - here
    return (here, (s, int(i != here), int(j != here))), (there, (s, int(j != there), int(i != there)))


def chunks():
    at = {place: tile for tile, place in PLACES.items()}
    return [
        [((*at[pair, q], m), g) for q in ((1, 0) if pair > 1 else (0, 1)) for g in range(2)]
        for pair in PAIRS
        for m in range(2)
    ]


def hops(a, b):
    ends = [(aux // AZ, aux % AZ, row // 2) for aux, row in (a, b)]
    far = [min((u - v) % n, (v - u) % n) for u, v, n in zip(*ends, (AX, AZ, CHIPS))]
    return sum(far) + 0.5 * (a[1] % 2 != b[1] % 2)


@functools.cache
def owners():
    to = {}
    for A in range(AX * AZ):
        X, j, h = A // 4, A // 2 % 2, A % 2
        for Y in range(CHIPS):
            for i in range(2):
                (core, tile), other = sources(X, j, Y, i)
                for g in range(2):
                    to.setdefault((Y, core, tile, g), []).append((1.0, (A, 2 * Y + i)))
                if other is not None:
                    to.setdefault((X, *other, h), []).append((MIRRORED, (A, 2 * Y + i)))
    return to


@functools.cache
def layout(Y, core):
    spots = [(x, m) for x in range(AX) for m in range(2)]

    def cost(piece, x, m, k):
        tile, g = piece
        at = (x * AZ + 2 * k + m, 2 * Y + core)
        return sum(w * hops(at, to) ** POWER for w, to in owners()[Y, core, tile, g])

    best = {0: (0.0, [])}
    for chunk in chunks():
        options = []
        for x, m in spots:
            table = [[cost(piece, x, m, k) for k in range(AZ // 2)] for piece in chunk]
            options.append(min((sum(table[p][k] for p, k in enumerate(order)), order) for order in itertools.permutations(range(AZ // 2))))
        after = {}
        for used, (total, chosen) in best.items():
            for n, (more, order) in enumerate(options):
                if not used >> n & 1:
                    found = (total + more, [*chosen, (*spots[n], order)])
                    now = used | 1 << n
                    if now not in after or found < after[now]:
                        after[now] = found
        best = after
    return best[2 ** len(spots) - 1][1]


def holder(Y, core, tile, g):
    for chunk, (x, m, order) in zip(chunks(), layout(Y, core)):
        if (tile, g) in chunk:
            return dev(x * AZ + 2 * order[chunk.index((tile, g))] + m, Y, core)


def summing_groups():
    rows = [(Y, c) for Y in range(CHIPS) for c in range(2)]
    first = [[dev(x * AZ + 2 * k + m, Y, c) for x, m, _ in layout(Y, c)] for k in range(AZ // 2) for Y, c in rows]
    second = [[dev(x * AZ + 2 * k + m, Y, c) for k in order] for Y, c in rows for x, m, order in layout(Y, c)]
    return first, second


def deliveries():
    direct = ([], [])
    mirrored = []
    for A in range(AX * AZ):
        X, j, h = A // 4, A // 2 % 2, A % 2
        for Y in range(CHIPS):
            for i in range(2):
                own, other = sources(X, j, Y, i)
                for p in range(2):
                    direct[p].append((holder(Y, *own, h ^ p), dev(A, Y, i)))
                if other is not None:
                    mirrored.append((holder(X, *other, h), dev(A, Y, i)))
    return direct[0], direct[1], mirrored


def local(slabs, significant):
    aux_here, occupied, cols = slabs.shape
    half = aux_here // 2
    depth = half * occupied
    row = lax.axis_index("row")
    aux = lax.axis_index("aux")
    chip, core = row // 2, row % 2

    blocks = cols // BS
    lane = lax.broadcasted_iota(jnp.int32, (1, cols), 1) // BS

    def mask_of(first, count, block_row):
        mine = lax.dynamic_slice(significant, (first, block_row * blocks), (count, blocks))
        return (jnp.where(lane == 0, mine[:, :1], mine[:, 1:2]) != 0)[:, None, :]

    def masked_half(x, block_row, which=core):
        x = x.reshape(half, occupied, cols)
        return jnp.where(mask_of(which * half, half, block_row), x, jnp.zeros_like(x)).reshape(depth, cols)

    def raw_half(which):
        return lax.dynamic_slice_in_dim(slabs, which * half, half, 0).reshape(depth, cols)

    swap = [(r, r ^ 1) for r in range(2 * CHIPS)]
    ring = [
        (2 * y + c, 2 * ((y + (1 if c == 0 else -1)) % CHIPS) + c)
        for y in range(CHIPS)
        for c in range(2)
    ]
    cross = [(2 * y + 1 - c, 2 * ((y + (1 if c == 0 else -1)) % CHIPS) + c) for y in range(CHIPS) for c in range(2)]
    a, b = lax.optimization_barrier((raw_half(core), raw_half(1 - core)))
    far_a, far_b = lax.ppermute(a, "row", ring), lax.ppermute(b, "row", cross)
    masked = jnp.where(mask_of(0, aux_here, row), slabs, jnp.zeros_like(slabs))
    own = masked_half(a, row)
    other = lax.ppermute(masked_half(b, row, 1 - core), "row", swap)
    left = (own.T, other.T)
    whole = masked.reshape(2 * depth, cols)

    def dot(x, y):
        return jnp.dot(x, y, preferred_element_type=jnp.float32)

    tiles = {(0, 0, 0): dot(whole.T, whole), (0, 0, 1): dot(left[0], other)}
    for step in range(1, CHIPS // 2 + 1):
        there = (chip + jnp.where(core == 0, CHIPS - step, step)) % CHIPS
        near_a = masked_half(far_a, 2 * there + core)
        near_b = masked_half(far_b, 2 * there + 1 - core)
        if step < CHIPS // 2:
            far_a, far_b = lax.ppermute(far_a, "row", ring), lax.ppermute(far_b, "row", ring)
            for e in range(2):
                tiles[step, e, 0], tiles[step, e, 1] = dot(left[e], near_a), dot(left[e], near_b)
        else:
            low = chip < CHIPS // 2
            tiles[4, 0, 0] = dot(jnp.where(low, left[0], left[1]), jnp.where(low, near_a, near_b))
            tiles[4, 0, 1] = dot(left[0], near_b)
    pieces = [tiles[tile] for chunk in chunks() for tile, g in chunk if g == 0]
    pieces = jnp.concatenate(pieces, axis=0).reshape(2 * AX, AZ // 2, BS, cols)

    first, second = summing_groups()
    got = lax.all_to_all(pieces, BOTH, 0, 0, axis_index_groups=first, tiled=True).sum(axis=0)
    got = lax.all_to_all(got, BOTH, 0, 0, axis_index_groups=second, tiled=True).sum(axis=0)

    near, next_to, mirrored = deliveries()
    t = lax.optimization_barrier(lax.ppermute(got, BOTH, mirrored).T)
    d0 = lax.ppermute(got, BOTH, near)
    d1 = lax.ppermute(got, BOTH, next_to)
    odd = aux % 2 == 1
    top = jnp.where(odd, d1[:, BS:], d0[:, :BS])
    bottom = jnp.where(odd, d0[:, BS:], d1[:, :BS])
    return jnp.concatenate([top, bottom], axis=0) + t


def solution(mesh):
    return jax.shard_map(
        local,
        mesh=mesh,
        in_specs=(P("aux", None, "row"), P("aux", None)),
        out_specs=P("row", "aux"),
        check_vma=False,
    )
```

```python
import functools
import itertools

import jax
import jax.numpy as jnp
from jax import lax
from jax.sharding import PartitionSpec as P

BS = 64
AX, AZ = 4, 8
CHIPS = 8
BOTH = ("aux", "row")


def dev(aux, chip, core):
    return aux * 2 * CHIPS + (chip % CHIPS) * 2 + core


TILES = [(0, 0, 0), (0, 0, 1)]
TILES += [(s, e, e ^ f) for s in range(1, CHIPS // 2) for f in range(2) for e in range(2)] + [(4, 0, 0), (4, 0, 1)]
POWER, MIRRORED = 2, 1.0


def sources(X, j, Y, i):
    d = (X - Y) % CHIPS
    if d == 0:
        return ((i, (0, 0, 0)), None) if i == j else ((i, (0, 0, 1)), (j, (0, 0, 1)))
    if d == CHIPS // 2:
        if i != j:
            return (i, (4, 0, 1)), (j, (4, 0, 1))
        low = Y < CHIPS // 2
        return (i if low else 1 - i, (4, 0, 0)), (1 - i if low else i, (4, 0, 0))
    s, here = (d, 1) if d < CHIPS // 2 else (CHIPS - d, 0)
    there = 1 - here
    return (here, (s, int(i != here), int(j != here))), (there, (s, int(j != there), int(i != there)))


def chunks():
    return [[(tile, n) for tile in TILES[k : k + 2] for n in range(2)] for k in range(0, len(TILES), 2)]


def hops(a, b):
    ends = [(aux // AZ, aux % AZ, row // 2) for aux, row in (a, b)]
    far = [min((u - v) % n, (v - u) % n) for u, v, n in zip(*ends, (AX, AZ, CHIPS))]
    return sum(far) + 0.5 * (a[1] % 2 != b[1] % 2)


@functools.cache
def owners():
    to = {}
    for A in range(AX * AZ):
        X, j, h = A // 4, A // 2 % 2, A % 2
        for Y in range(CHIPS):
            for i in range(2):
                (core, tile), other = sources(X, j, Y, i)
                to.setdefault((Y, core, tile, h), []).append((1.0, (A, 2 * Y + i)))
                if other is not None:
                    to.setdefault((X, *other, h), []).append((MIRRORED, (A, 2 * Y + i)))
    return to


@functools.cache
def layout(Y, core):
    spots = [(x, m) for x in range(AX) for m in range(2)]

    def cost(piece, x, m, k):
        tile, g = piece
        at = (x * AZ + 2 * k + m, 2 * Y + core)
        return sum(w * hops(at, to) ** POWER for w, to in owners()[Y, core, tile, g])

    best = {0: (0.0, [])}
    for chunk in chunks():
        options = []
        for x, m in spots:
            table = [[cost(piece, x, m, k) for k in range(AZ // 2)] for piece in chunk]
            options.append(min((sum(table[p][k] for p, k in enumerate(order)), order) for order in itertools.permutations(range(AZ // 2))))
        after = {}
        for used, (total, chosen) in best.items():
            for n, (more, order) in enumerate(options):
                if not used >> n & 1:
                    found = (total + more, [*chosen, (*spots[n], order)])
                    now = used | 1 << n
                    if now not in after or found < after[now]:
                        after[now] = found
        best = after
    return best[2 ** len(spots) - 1][1]


def holder(Y, core, tile, g):
    for chunk, (x, m, order) in zip(chunks(), layout(Y, core)):
        if (tile, g) in chunk:
            return dev(x * AZ + 2 * order[chunk.index((tile, g))] + m, Y, core)


def summing_groups():
    rows = [(Y, c) for Y in range(CHIPS) for c in range(2)]
    first = [[dev(x * AZ + 2 * k + m, Y, c) for x, m, _ in layout(Y, c)] for k in range(AZ // 2) for Y, c in rows]
    second = [[dev(x * AZ + 2 * k + m, Y, c) for k in order] for Y, c in rows for x, m, order in layout(Y, c)]
    return first, second


def deliveries():
    direct, mirrored = [], []
    for A in range(AX * AZ):
        X, j, h = A // 4, A // 2 % 2, A % 2
        for Y in range(CHIPS):
            for i in range(2):
                own, other = sources(X, j, Y, i)
                direct.append((holder(Y, *own, h), dev(A, Y, i)))
                if other is not None:
                    mirrored.append((holder(X, *other, h), dev(A, Y, i)))
    return direct, mirrored


def local(slabs, significant):
    aux_here, occupied, cols = slabs.shape
    half = aux_here // 2
    depth = half * occupied
    row = lax.axis_index("row")
    chip, core = row // 2, row % 2

    blocks = cols // BS
    lane = lax.broadcasted_iota(jnp.int32, (1, cols), 1) // BS

    def mask_of(first, count, block_row):
        mine = lax.dynamic_slice(significant, (first, block_row * blocks), (count, blocks))
        return (jnp.where(lane == 0, mine[:, :1], mine[:, 1:2]) != 0)[:, None, :]

    def masked_half(x, block_row, which=core):
        x = x.reshape(half, occupied, cols)
        return jnp.where(mask_of(which * half, half, block_row), x, jnp.zeros_like(x)).reshape(depth, cols)

    def raw_half(which):
        return lax.dynamic_slice_in_dim(slabs, which * half, half, 0).reshape(depth, cols)

    swap = [(r, r ^ 1) for r in range(2 * CHIPS)]
    ring = [
        (2 * y + c, 2 * ((y + (1 if c == 0 else -1)) % CHIPS) + c)
        for y in range(CHIPS)
        for c in range(2)
    ]
    cross = [(2 * y + 1 - c, 2 * ((y + (1 if c == 0 else -1)) % CHIPS) + c) for y in range(CHIPS) for c in range(2)]
    a, b = lax.optimization_barrier((raw_half(core), raw_half(1 - core)))
    far_a, far_b = lax.ppermute(a, "row", ring), lax.ppermute(b, "row", cross)
    masked = jnp.where(mask_of(0, aux_here, row), slabs, jnp.zeros_like(slabs))
    own = masked_half(a, row)
    other = lax.ppermute(masked_half(b, row, 1 - core), "row", swap)
    left = (own.T, other.T)
    whole = masked.reshape(2 * depth, cols)

    def dot(x, y):
        return jnp.dot(x, y, preferred_element_type=jnp.float32)

    tiles = {(0, 0, 0): dot(whole.T, whole), (0, 0, 1): dot(left[0], other)}
    for step in range(1, CHIPS // 2 + 1):
        there = (chip + jnp.where(core == 0, CHIPS - step, step)) % CHIPS
        near_a = masked_half(far_a, 2 * there + core)
        near_b = masked_half(far_b, 2 * there + 1 - core)
        if step < CHIPS // 2:
            far_a, far_b = lax.ppermute(far_a, "row", ring), lax.ppermute(far_b, "row", ring)
            for e in range(2):
                tiles[step, e, 0], tiles[step, e, 1] = dot(left[e], near_a), dot(left[e], near_b)
        else:
            low = chip < CHIPS // 2
            tiles[4, 0, 0] = dot(jnp.where(low, left[0], left[1]), jnp.where(low, near_a, near_b))
            tiles[4, 0, 1] = dot(left[0], near_b)
    pieces = jnp.concatenate([tiles[tile] for tile in TILES], axis=0).reshape(2 * AX, 2 * cols, cols)

    first, second = summing_groups()
    got = lax.all_to_all(pieces, BOTH, 0, 0, axis_index_groups=first, tiled=True).sum(axis=0)
    got = got.reshape(2, 2, BS, cols)
    packed = [jnp.concatenate([got[:, 0, :, n * BS : (n + 1) * BS], got[:, 1, :, n * BS : (n + 1) * BS]], axis=2) for n in range(2)]
    got = jnp.concatenate([got, jnp.stack(packed, axis=1)], axis=2).reshape(4, cols, cols)
    got = lax.all_to_all(got, BOTH, 0, 0, axis_index_groups=second, tiled=True).sum(axis=0)

    direct, mirrored = deliveries()
    t = lax.ppermute(got[:BS], BOTH, mirrored).T
    d = lax.ppermute(got[BS:], BOTH, direct)
    return jnp.concatenate([d[:, :BS], d[:, BS:]], axis=0) + t


def solution(mesh):
    return jax.shard_map(
        local,
        mesh=mesh,
        in_specs=(P("aux", None, "row"), P("aux", None)),
        out_specs=P("row", "aux"),
        check_vma=False,
    )
```

```python
import functools
import itertools

import jax
import jax.numpy as jnp
from jax import lax
from jax.sharding import PartitionSpec as P

BS = 64
AX, AZ = 4, 8
CHIPS = 8
BOTH = ("aux", "row")


def dev(aux, chip, core):
    return aux * 2 * CHIPS + (chip % CHIPS) * 2 + core


PLACES = {(0, 0): (0, 0), (1, 1): (0, 1), (2, 1): (1, 0), (3, 1): (1, 1)}
PLACES |= {(4, 0): (2, 0), (3, 0): (2, 1), (2, 0): (3, 0), (1, 0): (3, 1)}
PAIRS = [0, 3, 1, 2]
POWER, MIRRORED = 2, 1.25


def sources(X, j, Y, i):
    d = (X - Y) % CHIPS
    if d == 0:
        return ((i, (0, 0, 0)), None) if i == j else ((i, (0, 0, 1)), (j, (0, 0, 1)))
    if d == CHIPS // 2:
        if i != j:
            return (i, (4, 0, 1)), (j, (4, 0, 1))
        low = Y < CHIPS // 2
        return (i if low else 1 - i, (4, 0, 0)), (1 - i if low else i, (4, 0, 0))
    s, here = (d, 1) if d < CHIPS // 2 else (CHIPS - d, 0)
    there = 1 - here
    return (here, (s, int(i != here), int(j != here))), (there, (s, int(j != there), int(i != there)))


def chunks():
    at = {place: tile for tile, place in PLACES.items()}
    return [
        [((*at[pair, q], m), g) for q in ((1, 0) if pair > 1 else (0, 1)) for g in range(2)]
        for pair in PAIRS
        for m in range(2)
    ]


def hops(a, b):
    ends = [(aux // AZ, aux % AZ, row // 2) for aux, row in (a, b)]
    far = [min((u - v) % n, (v - u) % n) for u, v, n in zip(*ends, (AX, AZ, CHIPS))]
    return sum(far) + 0.5 * (a[1] % 2 != b[1] % 2)


@functools.cache
def owners():
    to = {}
    for A in range(AX * AZ):
        X, j, h = A // 4, A // 2 % 2, A % 2
        for Y in range(CHIPS):
            for i in range(2):
                (core, tile), other = sources(X, j, Y, i)
                for g in range(2):
                    to.setdefault((Y, core, tile, g), []).append((1.0, (A, 2 * Y + i)))
                if other is not None:
                    to.setdefault((X, *other, h), []).append((MIRRORED, (A, 2 * Y + i)))
    return to


@functools.cache
def layout(Y, core):
    spots = [(x, m) for x in range(AX) for m in range(2)]

    def cost(piece, x, m, k):
        tile, g = piece
        at = (x * AZ + 2 * k + m, 2 * Y + core)
        return sum(w * hops(at, to) ** POWER for w, to in owners()[Y, core, tile, g])

    best = {0: (0.0, [])}
    for chunk in chunks():
        options = []
        for x, m in spots:
            table = [[cost(piece, x, m, k) for k in range(AZ // 2)] for piece in chunk]
            options.append(min((sum(table[p][k] for p, k in enumerate(order)), order) for order in itertools.permutations(range(AZ // 2))))
        after = {}
        for used, (total, chosen) in best.items():
            for n, (more, order) in enumerate(options):
                if not used >> n & 1:
                    found = (total + more, [*chosen, (*spots[n], order)])
                    now = used | 1 << n
                    if now not in after or found < after[now]:
                        after[now] = found
        best = after
    return best[2 ** len(spots) - 1][1]


def holder(Y, core, tile, g):
    for chunk, (x, m, order) in zip(chunks(), layout(Y, core)):
        if (tile, g) in chunk:
            return dev(x * AZ + 2 * order[chunk.index((tile, g))] + m, Y, core)


def summing_groups():
    rows = [(Y, c) for Y in range(CHIPS) for c in range(2)]
    first = [[dev(x * AZ + 2 * k + m, Y, c) for x, m, _ in layout(Y, c)] for k in range(AZ // 2) for Y, c in rows]
    second = [[dev(x * AZ + 2 * k + m, Y, c) for k in order] for Y, c in rows for x, m, order in layout(Y, c)]
    return first, second


def deliveries():
    direct = ([], [])
    mirrored = []
    for A in range(AX * AZ):
        X, j, h = A // 4, A // 2 % 2, A % 2
        for Y in range(CHIPS):
            for i in range(2):
                own, other = sources(X, j, Y, i)
                for p in range(2):
                    direct[p].append((holder(Y, *own, h ^ p), dev(A, Y, i)))
                if other is not None:
                    mirrored.append((holder(X, *other, h), dev(A, Y, i)))
    return direct[0], direct[1], mirrored


def local(slabs, significant):
    aux_here, occupied, cols = slabs.shape
    half = aux_here // 2
    depth = half * occupied
    row = lax.axis_index("row")
    aux = lax.axis_index("aux")
    chip, core = row // 2, row % 2

    blocks = cols // BS
    lane = lax.broadcasted_iota(jnp.int32, (1, cols), 1) // BS

    def mask_of(first, count, block_row):
        mine = lax.dynamic_slice(significant, (first, block_row * blocks), (count, blocks))
        return (jnp.where(lane == 0, mine[:, :1], mine[:, 1:2]) != 0)[:, None, :]

    def masked_half(x, block_row, which=core):
        x = x.reshape(half, occupied, cols)
        return jnp.where(mask_of(which * half, half, block_row), x, jnp.zeros_like(x)).reshape(depth, cols)

    def raw_half(which):
        return lax.dynamic_slice_in_dim(slabs, which * half, half, 0).reshape(depth, cols)

    swap = [(r, r ^ 1) for r in range(2 * CHIPS)]
    ring = [
        (2 * y + c, 2 * ((y + (1 if c == 0 else -1)) % CHIPS) + c)
        for y in range(CHIPS)
        for c in range(2)
    ]
    cross = [(2 * y + 1 - c, 2 * ((y + (1 if c == 0 else -1)) % CHIPS) + c) for y in range(CHIPS) for c in range(2)]
    a, b = lax.optimization_barrier((raw_half(core), raw_half(1 - core)))
    far_a, far_b = lax.ppermute(a, "row", ring), lax.ppermute(b, "row", cross)
    masked = jnp.where(mask_of(0, aux_here, row), slabs, jnp.zeros_like(slabs))
    own = masked_half(a, row)
    other = lax.ppermute(masked_half(b, row, 1 - core), "row", swap)
    left = (own.T, other.T)
    whole = masked.reshape(2 * depth, cols)

    def dot(x, y):
        return jnp.dot(x, y, preferred_element_type=jnp.float32)

    tiles = {(0, 0, 0): dot(whole.T, whole), (0, 0, 1): dot(left[0], other)}
    for step in range(1, CHIPS // 2 + 1):
        there = (chip + jnp.where(core == 0, CHIPS - step, step)) % CHIPS
        near_a = masked_half(far_a, 2 * there + core)
        near_b = masked_half(far_b, 2 * there + 1 - core)
        if step < CHIPS // 2:
            far_a, far_b = lax.ppermute(far_a, "row", ring), lax.ppermute(far_b, "row", ring)
            for e in range(2):
                tiles[step, e, 0], tiles[step, e, 1] = dot(left[e], near_a), dot(left[e], near_b)
        else:
            low = chip < CHIPS // 2
            tiles[4, 0, 0] = dot(jnp.where(low, left[0], left[1]), jnp.where(low, near_a, near_b))
            tiles[4, 0, 1] = dot(left[0], near_b)
    pieces = [tiles[tile] for chunk in chunks() for tile, g in chunk if g == 0]
    pieces = jnp.concatenate(pieces, axis=0).reshape(2 * AX, AZ // 2, BS, cols)

    first, second = summing_groups()
    got = lax.all_to_all(pieces, BOTH, 0, 0, axis_index_groups=first, tiled=True).sum(axis=0)
    got = lax.all_to_all(got, BOTH, 0, 0, axis_index_groups=second, tiled=True).sum(axis=0)

    near, next_to, mirrored = deliveries()
    t = lax.optimization_barrier(lax.ppermute(got, BOTH, mirrored).T)
    d0 = lax.ppermute(got, BOTH, near)
    d1 = lax.ppermute(got, BOTH, next_to)
    odd = aux % 2 == 1
    top = jnp.where(odd, d1[:, BS:], d0[:, :BS])
    bottom = jnp.where(odd, d0[:, BS:], d1[:, :BS])
    return jnp.concatenate([top, bottom], axis=0) + t


def solution(mesh):
    return jax.shard_map(
        local,
        mesh=mesh,
        in_specs=(P("aux", None, "row"), P("aux", None)),
        out_specs=P("row", "aux"),
        check_vma=False,
    )
```
